32 devices in a mesh: grp: 2 (over y), tm: 4 (over x, core), chan: 4 (over z).
Axes of the slice: x: 2, y: 2, z: 4, core: 2. Of those that a mesh axis runs over, the one named last changes fastest.
Arguments:
- records: bfloat16 [512, 3, 1024], P(('grp', 'tm', 'chan')), parts along dimension 0, may hold values from -6 to 6
- templates: bfloat16 [256, 3, 200, 256], P(('tm', 'chan')), may hold values from -6 to 6
- moveouts: int32 [256, 3], P(('tm', 'chan')), may hold values from 0 to 999
- uptime: int32 [512, 2], P(('grp', 'tm', 'chan')), parts along dimension 0, may hold values from 0 to 512
Outputs:
- cccsum: float32 [256, 2048], P(None, ('grp', 'tm', 'chan')), parts along dimension 1
The draws below stay inside these ranges and needn't reach their ends.
There are 2 independent parts, one for each index of `grp`. The reference program is written for one: setup_inputs(seed, part) draws one part's arguments, and reference() takes and returns one part's arrays. A program takes and returns all parts, laid end to end along the dimension named above; an argument that names none is the same for every part. Nothing has to cross between parts.
All inputs are finite; a program needn't handle non-finite values.
Results may differ from the reference program's by a relative error of at most 0.0041.
Values may be sent and summed in bfloat16 or wider, within the bound.
A program may use at most 64 MiB of HBM per device.

```python
import jax
import jax.numpy as jnp
from jax import lax

STATIONS = 256
COMP = 3
TLEN = 200
TEMPLATES = 256
MAXMO = 1000
BLK = 512
NS = 1024
NBLK = 2


def draw_moveouts(key, part):
    first_key, second_key = jax.random.split(key)
    values = jax.random.randint(first_key, (STATIONS * COMP,), 0, MAXMO, dtype=jnp.int32)
    chosen = jax.random.permutation(second_key, STATIONS * COMP)
    values = values.at[chosen[0]].set(MAXMO - 1)
    values = values.at[chosen[1]].set(0)
    return values.reshape(STATIONS, COMP).astype(jnp.int32)


def draw_uptime(key, part):
    first_key, second_key = jax.random.split(jax.random.fold_in(key, 7))
    counts = jax.random.randint(first_key, (STATIONS * NBLK,), 0, 2 * BLK, dtype=jnp.int32)
    counts = jnp.minimum(counts, BLK)
    chosen = jax.random.permutation(second_key, STATIONS * NBLK)
    counts = counts.at[chosen[0]].set(0)
    counts = counts.at[chosen[1]].set(BLK)
    return counts.reshape(STATIONS, NBLK).astype(jnp.int32)


def block_levels(stream_key, extent, pieces, least, top_value):
    def one(dim, parts):
        draws = jax.random.uniform(jax.random.fold_in(jax.random.fold_in(stream_key, 6), dim), (parts,), jnp.float32, least / len(pieces), top_value / len(pieces))
        return jnp.repeat(jnp.exp(draws), extent[dim] // parts).reshape((-1,) + (1,) * (len(extent) - dim - 1))

    level = one(*pieces[0])
    for cut in pieces[1:]:
        level = level * one(*cut)
    return level


def gaussian(key, shape, scale, bound, pieces=(), kind=jnp.bfloat16):
    entries = scale * jax.random.normal(key, shape, jnp.float32)
    if pieces:
        entries = entries * block_levels(key, shape, pieces, -0.22, 0.18)
    return jnp.clip(entries, -bound, bound).astype(kind)


def setup_inputs(seed: int = 0, part: int = 0) -> dict:
    keys = jax.random.split(jax.random.key(seed), 5)
    part_splits = jax.random.split(jax.random.fold_in(keys[4], part), 5)
    records = gaussian(part_splits[0], (STATIONS, COMP, NS), 1.0, 6.0, ((0, 16),))
    templates = gaussian(keys[1], (STATIONS, COMP, TLEN, TEMPLATES), 1.0, 6.0, ((0, 16),))
    moveouts = draw_moveouts(jax.random.fold_in(keys[4], 71), part)
    uptime = draw_uptime(jax.random.fold_in(jax.random.fold_in(keys[4], part), 71), part)
    return dict(records=records, templates=templates, moveouts=moveouts, uptime=uptime)


def prepare_records(records, moveouts, uptime):
    stations, components, length = records.shape
    block_count = uptime.shape[1]
    offsets = lax.broadcasted_iota(jnp.int32, (block_count, length // block_count), 1)
    live_mask = (offsets[None, :, :] < uptime[:, :, None]).reshape(stations, 1, length)
    masked = jnp.where(live_mask, records, jnp.zeros((), records.dtype))
    padded = jnp.concatenate([masked, jnp.zeros((stations, components, MAXMO), records.dtype)], axis=2)
    flat_rows = padded.reshape(stations * components, length + MAXMO)
    starts = moveouts.reshape(stations * components).astype(jnp.int32)

    def slice_row(record_row, start_at):
        return lax.dynamic_slice_in_dim(record_row, start_at, length)
    shifted = jax.vmap(slice_row)(flat_rows, starts)
    return shifted.reshape(stations, components, length)

def normalize_templates(templates):
    values = templates.astype(jnp.float32)
    squares = lax.optimization_barrier(jnp.sum(values * values, axis=2, keepdims=True))
    return (values * lax.rsqrt(squares + 1e-06)).astype(jnp.bfloat16)

def correlate_station(station_rows, unit_rows):
    channels, length = station_rows.shape
    window_len = unit_rows.shape[1]
    out_len = length - window_len + 1
    tiled_rows = jnp.tile(station_rows, (1, window_len + 1))[:, :window_len * (length + 1)]
    windows = tiled_rows.reshape(channels, window_len, length + 1)[:, :, :out_len]
    energy = lax.optimization_barrier(jnp.sum(jnp.square(windows.astype(jnp.float32)), axis=1))
    factor = lax.rsqrt(jnp.maximum(energy, 1.0))
    scaled = (windows.astype(jnp.float32) * factor[:, None, :]).astype(jnp.bfloat16)
    unit_flat = unit_rows.reshape(channels * window_len, unit_rows.shape[2])
    return jnp.dot(unit_flat.T, scaled.reshape(channels * window_len, out_len), preferred_element_type=jnp.float32)

def reference(records, templates, moveouts, uptime):
    shifted = prepare_records(records, moveouts, uptime)
    unit_bank = normalize_templates(templates)
    padded = jnp.concatenate([shifted, jnp.zeros((STATIONS, COMP, TLEN - 1), shifted.dtype)], axis=2)

    def station_step(running, station_data):
        station_rows, unit_rows = station_data
        return (running + correlate_station(station_rows, unit_rows), None)
    initial = jnp.zeros((TEMPLATES, NS), jnp.float32)
    result, ignored = lax.scan(station_step, initial, (padded, unit_bank))
    return result
```

```python
import functools

import jax
import jax.numpy as jnp
from jax import lax
from jax.experimental import pallas as pl
from jax.experimental.pallas import tpu as pltpu
from jax.sharding import PartitionSpec as P

LANES = 128
SUBS = 8


def roll_left(value, amount):
    size = value.shape[-1]
    return pltpu.roll(value, (size - amount) % size, axis=1)


def windowed_sum(squares, window_len):
    total, covered, power, width = None, 0, squares, 1
    while width <= window_len:
        if window_len & width:
            piece = power if covered == 0 else roll_left(power, covered)
            total = piece if total is None else total + piece
            covered += width
        if 2 * width <= window_len:
            power = power + roll_left(power, width)
        width *= 2
    return total


def correlate_kernel(moveouts, uptime, records, templates, out, rows, windows, units, total):
    step = pl.program_id(0)
    _, components, length = records.shape
    window_len = templates.shape[2]
    depth = units.shape[0] // components
    padded = rows.shape[1]
    block_count = uptime.shape[1]
    block_len = length // block_count

    @pl.when(step == 0)
    def _():
        rows[...] = jnp.zeros_like(rows)
        units[...] = jnp.zeros_like(units)
        total[...] = jnp.zeros_like(total)

    time = lax.broadcasted_iota(jnp.int32, (1, length), 1)
    limit = jnp.zeros((1, length), jnp.int32)
    for block in range(block_count):
        limit = jnp.where(time >= block * block_len, block * block_len + uptime[step, block], limit)
    for comp in range(components):
        row = records[0, comp:comp + 1, :].astype(jnp.float32)
        row = jnp.where(time < limit, row, 0.0)
        start = moveouts[step, comp]
        row = pltpu.roll(row, lax.rem(length - start, length), axis=1)
        rows[comp:comp + 1, :length] = jnp.where(time < length - start, row, 0.0)

    signal = rows[...]
    energy = windowed_sum(signal * signal, window_len)
    factor = lax.rsqrt(jnp.maximum(energy[:, :length], 1.0)).T

    sub = lax.broadcasted_iota(jnp.int32, (SUBS, padded), 0)
    for comp in range(components):
        values = templates[0, comp].astype(jnp.float32)
        squares = jnp.sum(values * values, axis=0, keepdims=True)
        unit = (values * lax.rsqrt(squares + 1e-06)).astype(jnp.bfloat16)
        units[comp * depth:comp * depth + window_len, :] = unit

        base = jnp.broadcast_to(rows[comp:comp + 1, :], (SUBS, padded))
        for bit in (1, 2, 4):
            base = jnp.where((sub & bit) != 0, roll_left(base, bit), base)
        for pair in range(LANES // (2 * SUBS)):
            first = base if pair == 0 else roll_left(base, 2 * SUBS * pair)
            second = roll_left(base, 2 * SUBS * pair + SUBS)
            both = jnp.concatenate([first, second], axis=0)
            for chunk in range(length // LANES):
                top = chunk * LANES + 2 * SUBS * pair
                scale = factor[top:top + 2 * SUBS, comp:comp + 1]
                window = both[:, chunk * LANES:chunk * LANES + depth]
                windows[top:top + 2 * SUBS, comp * depth:(comp + 1) * depth] = (
                    window * scale
                ).astype(jnp.bfloat16)

    total[...] += jnp.dot(windows[...], units[...], preferred_element_type=jnp.float32)

    @pl.when(step == pl.num_programs(0) - 1)
    def _():
        out[...] = total[...].astype(out.dtype)


def correlate(records, templates, moveouts, uptime):
    stations, components, length = records.shape
    _, _, window_len, bank = templates.shape
    depth = pl.cdiv(window_len, LANES) * LANES
    padded = length + depth
    return pl.pallas_call(
        correlate_kernel,
        out_shape=jax.ShapeDtypeStruct((length, bank), jnp.float32),
        grid_spec=pltpu.PrefetchScalarGridSpec(
            num_scalar_prefetch=2,
            grid=(stations,),
            in_specs=[
                pl.BlockSpec((1, components, length), lambda s, *_: (s, 0, 0)),
                pl.BlockSpec((1, components, window_len, bank), lambda s, *_: (s, 0, 0, 0)),
            ],
            out_specs=pl.BlockSpec((length, bank), lambda s, *_: (0, 0)),
            scratch_shapes=[
                pltpu.VMEM((SUBS, padded), jnp.float32),
                pltpu.VMEM((length, components * depth), jnp.bfloat16),
                pltpu.VMEM((components * depth, bank), jnp.bfloat16),
                pltpu.VMEM((length, bank), jnp.float32),
            ],
        ),
        name="correlate",
    )(moveouts, uptime, records, templates)


def body(records, templates, moveouts, uptime):
    partial = correlate(records, templates, moveouts, uptime)
    mine = lax.psum_scatter(partial, ("tm", "chan"), scatter_dimension=0, tiled=True)
    return mine.T


def solution(mesh):
    placed = (
        P(("grp", "tm", "chan"), None, None),
        P(("tm", "chan"), None, None, None),
        P(("tm", "chan"), None),
        P(("grp", "tm", "chan"), None),
    )
    return jax.shard_map(
        body, mesh=mesh, in_specs=placed, out_specs=P(None, ("grp", "tm", "chan")), check_vma=False
    )
```

```python
import functools

import jax
import jax.numpy as jnp
from jax import lax
from jax.experimental import pallas as pl
from jax.experimental.pallas import tpu as pltpu
from jax.sharding import PartitionSpec as P

LANES = 128
SUBS = 8


def roll_left(value, amount):
    size = value.shape[-1]
    return pltpu.roll(value, (size - amount) % size, axis=1)


def windowed_sum(squares, window_len):
    total, covered, power, width = None, 0, squares, 1
    while width <= window_len:
        if window_len & width:
            piece = power if covered == 0 else roll_left(power, covered)
            total = piece if total is None else total + piece
            covered += width
        if 2 * width <= window_len:
            power = power + roll_left(power, width)
        width *= 2
    return total


def correlate_kernel(blocks, counts, records, templates, out, traces, rows, windows, units, total):
    step = pl.program_id(0)
    components, _, length = records.shape
    window_len = templates.shape[2]
    depth = units.shape[0] // components
    padded = rows.shape[1]
    block_len = length // blocks

    @pl.when(step == 0)
    def _():
        traces[...] = records[...].astype(jnp.float32)
        rows[...] = jnp.zeros_like(rows)
        units[...] = jnp.zeros_like(units)
        total[...] = jnp.zeros_like(total)

    time = lax.broadcasted_iota(jnp.int32, (1, length), 1)
    limit = jnp.zeros((1, length), jnp.int32)
    for block in range(blocks):
        limit = jnp.where(time >= block * block_len, block * block_len + counts[components + block, step], limit)
    for comp in range(components):
        row = jnp.where(time < limit, traces[comp, pl.ds(step, 1), :], 0.0)
        start = counts[comp, step]
        row = pltpu.roll(row, lax.rem(length - start, length), axis=1)
        rows[comp:comp + 1, :length] = jnp.where(time < length - start, row, 0.0)

    signal = rows[...]
    energy = windowed_sum(signal * signal, window_len)
    factor = lax.rsqrt(jnp.maximum(energy[:, :length], 1.0)).T

    sub = lax.broadcasted_iota(jnp.int32, (SUBS, padded), 0)
    for comp in range(components):
        values = templates[0, comp].astype(jnp.float32)
        squares = jnp.sum(values * values, axis=0, keepdims=True)
        unit = (values * lax.rsqrt(squares + 1e-06)).astype(jnp.bfloat16)
        units[comp * depth:comp * depth + window_len, :] = unit

        base = jnp.broadcast_to(rows[comp:comp + 1, :], (SUBS, padded))
        for bit in (1, 2, 4):
            base = jnp.where((sub & bit) != 0, roll_left(base, bit), base)
        for pair in range(LANES // (2 * SUBS)):
            first = base if pair == 0 else roll_left(base, 2 * SUBS * pair)
            second = roll_left(base, 2 * SUBS * pair + SUBS)
            both = jnp.concatenate([first, second], axis=0)
            for chunk in range(length // LANES):
                top = chunk * LANES + 2 * SUBS * pair
                scale = factor[top:top + 2 * SUBS, comp:comp + 1]
                window = both[:, chunk * LANES:chunk * LANES + depth]
                windows[top:top + 2 * SUBS, comp * depth:(comp + 1) * depth] = (
                    window * scale
                ).astype(jnp.bfloat16)

    total[...] += jnp.dot(windows[...], units[...], preferred_element_type=jnp.float32)

    @pl.when(step == pl.num_programs(0) - 1)
    def _():
        out[...] = total[...].astype(out.dtype)


def correlate(records, templates, moveouts, uptime):
    stations, components, length = records.shape
    _, _, window_len, bank = templates.shape
    depth = pl.cdiv(window_len, LANES) * LANES
    padded = length + depth
    counts = jnp.concatenate([moveouts.T, uptime.T], axis=0)
    return pl.pallas_call(
        functools.partial(correlate_kernel, uptime.shape[1]),
        out_shape=jax.ShapeDtypeStruct((length, bank), jnp.float32),
        grid_spec=pltpu.PrefetchScalarGridSpec(
            num_scalar_prefetch=1,
            grid=(stations,),
            in_specs=[
                pl.BlockSpec((components, stations, length), lambda s, *_: (0, 0, 0)),
                pl.BlockSpec((1, components, window_len, bank), lambda s, *_: (s, 0, 0, 0)),
            ],
            out_specs=pl.BlockSpec((length, bank), lambda s, *_: (0, 0)),
            scratch_shapes=[
                pltpu.VMEM((components, stations, length), jnp.float32),
                pltpu.VMEM((SUBS, padded), jnp.float32),
                pltpu.VMEM((length, components * depth), jnp.bfloat16),
                pltpu.VMEM((components * depth, bank), jnp.bfloat16),
                pltpu.VMEM((length, bank), jnp.float32),
            ],
        ),
        name="correlate",
    )(counts, records.transpose(1, 0, 2), templates)


def reduce_kernel(
    x_size, z_size, part, out, from_core, to_x, from_x, to_z, from_z,
    core_send, core_recv, x_send, x_recv, z_send, z_recv,
):
    tm, z = lax.axis_index("tm"), lax.axis_index("chan")
    x, core = lax.div(tm, 2), lax.rem(tm, 2)
    rows = part.shape[0] // (2 * x_size)
    piece = rows // z_size
    mesh_id = pl.DeviceIdType.MESH
    partner = 1 - core + 2 * x

    barrier = pltpu.get_barrier_semaphore()
    pl.semaphore_signal(barrier, inc=1, device_id={"tm": partner}, device_id_type=mesh_id)
    for d in range(1, x_size):
        peer = 2 * lax.rem(x + d, x_size) + core
        pl.semaphore_signal(barrier, inc=1, device_id={"tm": peer}, device_id_type=mesh_id)
    for e in range(1, z_size):
        peer = lax.rem(z + e, z_size)
        pl.semaphore_signal(barrier, inc=1, device_id={"chan": peer}, device_id_type=mesh_id)
    pl.semaphore_wait(barrier, x_size + z_size - 1)

    def start(src, dst, send, recv, device):
        copy = pltpu.make_async_remote_copy(
            src_ref=src, dst_ref=dst, send_sem=send, recv_sem=recv,
            device_id=device, device_id_type=mesh_id,
        )
        copy.start()
        return copy

    core_copies, x_copies, z_copies = [], [], []
    for d in range(1, x_size + 1):
        peer = lax.rem(x + d, x_size)
        first = pl.multiple_of((2 * peer + 1 - core) * rows, rows)
        core_copies.append(start(
            part.at[pl.ds(first, rows)], from_core.at[d - 1],
            core_send.at[d - 1], core_recv.at[d - 1], {"tm": partner},
        ))

    for d in range(1, x_size):
        peer = lax.rem(x + d, x_size)
        core_copies[d - 1].wait_recv()
        pending = []
        for e in range(1, z_size + 1):
            offset = pl.multiple_of(lax.rem(z + e, z_size) * piece, piece)
            first = pl.multiple_of((2 * peer + core) * rows + offset, piece)
            value = part[pl.ds(first, piece), :] + from_core[d - 1, pl.ds(offset, piece), :]
            to_x[d - 1, pl.ds(offset, piece), :] = value.astype(to_x.dtype)
            pending.append(start(
                to_x.at[d - 1, pl.ds(offset, piece)], from_x.at[d - 1, pl.ds(offset, piece)],
                x_send.at[d - 1, e - 1], x_recv.at[d - 1, e - 1], {"tm": 2 * peer + core},
            ))
        x_copies.append(pending)

    core_copies[x_size - 1].wait_recv()
    for e in range(1, z_size + 1):
        peer = lax.rem(z + e, z_size)
        offset = pl.multiple_of(peer * piece, piece)
        first = pl.multiple_of(tm * rows + offset, piece)
        value = part[pl.ds(first, piece), :] + from_core[x_size - 1, pl.ds(offset, piece), :]
        for d in range(1, x_size):
            x_copies[d - 1][e - 1].wait_recv()
            value = value + from_x[d - 1, pl.ds(offset, piece), :].astype(jnp.float32)
        if e < z_size:
            to_z[e - 1] = value.astype(to_z.dtype)
            z_copies.append(start(
                to_z.at[e - 1], from_z.at[e - 1], z_send.at[e - 1], z_recv.at[e - 1],
                {"chan": peer},
            ))
    for e in range(1, z_size):
        z_copies[e - 1].wait_recv()
        value = value + from_z[e - 1].astype(jnp.float32)
    out[...] = value

    for copy in core_copies + [c for pending in x_copies for c in pending] + z_copies:
        copy.wait_send()


def reduce_scatter(part):
    x_size, z_size = lax.axis_size("tm") // 2, lax.axis_size("chan")
    length, bank = part.shape
    rows = length // (2 * x_size)
    piece = rows // z_size
    others_x, others_z = max(x_size - 1, 1), max(z_size - 1, 1)
    dma = pltpu.SemaphoreType.DMA
    return pl.pallas_call(
        functools.partial(reduce_kernel, x_size, z_size),
        out_shape=jax.ShapeDtypeStruct((piece, bank), jnp.float32),
        in_specs=[pl.BlockSpec(memory_space=pltpu.VMEM)],
        out_specs=pl.BlockSpec(memory_space=pltpu.VMEM),
        scratch_shapes=[
            pltpu.VMEM((x_size, rows, bank), jnp.float32),
            pltpu.VMEM((others_x, rows, bank), jnp.bfloat16),
            pltpu.VMEM((others_x, rows, bank), jnp.bfloat16),
            pltpu.VMEM((others_z, piece, bank), jnp.bfloat16),
            pltpu.VMEM((others_z, piece, bank), jnp.bfloat16),
            dma((x_size,)), dma((x_size,)),
            dma((others_x, z_size)), dma((others_x, z_size)),
            dma((others_z,)), dma((others_z,)),
        ],
        compiler_params=pltpu.CompilerParams(collective_id=0, has_side_effects=True),
        name="reduce_scatter",
    )(part)


def body(records, templates, moveouts, uptime):
    return reduce_scatter(correlate(records, templates, moveouts, uptime)).T


def solution(mesh):
    placed = (
        P(("grp", "tm", "chan"), None, None),
        P(("tm", "chan"), None, None, None),
        P(("tm", "chan"), None),
        P(("grp", "tm", "chan"), None),
    )
    return jax.shard_map(
        body, mesh=mesh, in_specs=placed, out_specs=P(None, ("grp", "tm", "chan")), check_vma=False
    )
```

```python
import functools

import jax
import jax.numpy as jnp
from jax import lax
from jax.experimental import pallas as pl
from jax.experimental.pallas import tpu as pltpu
from jax.sharding import PartitionSpec as P

LANES = 128
SUBS = 8
ROT = jnp.bfloat16


def roll_left(value, amount):
    size = value.shape[-1]
    return pltpu.roll(value, (size - amount) % size, axis=1)


def windowed_sum(squares, window_len):
    total, covered, power, width = None, 0, squares, 1
    while width <= window_len:
        if window_len & width:
            piece = power if covered == 0 else roll_left(power, covered)
            total = piece if total is None else total + piece
            covered += width
        if 2 * width <= window_len:
            power = power + roll_left(power, width)
        width *= 2
    return total


def correlate_kernel(blocks, counts, records, templates, out, traces, rows, windows, units, total):
    step = pl.program_id(0)
    components, _, length = records.shape
    window_len = templates.shape[2]
    depth = units.shape[1] // components
    padded = rows.shape[1]
    block_len = length // blocks

    @pl.when(step == 0)
    def _():
        traces[...] = records[...].astype(jnp.float32)
        rows[...] = jnp.zeros_like(rows)
        windows[...] = jnp.zeros_like(windows)
        total[...] = jnp.zeros_like(total)

    time = lax.broadcasted_iota(jnp.int32, (1, length), 1)
    limit = jnp.zeros((1, length), jnp.int32)
    for block in range(blocks):
        limit = jnp.where(time >= block * block_len, block * block_len + counts[components + block, step], limit)
    for comp in range(components):
        row = jnp.where(time < limit, traces[comp, pl.ds(step, 1), :], 0.0)
        start = counts[comp, step]
        row = pltpu.roll(row, lax.rem(length - start, length), axis=1)
        rows[comp:comp + 1, :length] = jnp.where(time < length - start, row, 0.0)

    signal = rows[...]
    energy = windowed_sum(signal * signal, window_len)
    factor = lax.rsqrt(jnp.maximum(energy[:, :length], 1.0))

    sub = lax.broadcasted_iota(jnp.int32, (SUBS, padded), 0)
    for comp in range(components):
        values = templates[0, comp].astype(jnp.float32)
        squares = jnp.sum(values * values, axis=0, keepdims=True)
        unit = (values * lax.rsqrt(squares + 1e-06)).astype(jnp.bfloat16)
        blank = jnp.zeros((depth - window_len, unit.shape[1]), unit.dtype)
        units[:, comp * depth:(comp + 1) * depth] = jnp.concatenate([unit, blank], axis=0).T

        base = jnp.broadcast_to(rows[comp:comp + 1, :], (SUBS, padded))
        for bit in (1, 2, 4):
            base = jnp.where((sub & bit) != 0, roll_left(base, bit), base)
        both = jnp.concatenate([base, roll_left(base, SUBS)], axis=0).astype(ROT)
        scale = jnp.broadcast_to(factor[comp:comp + 1, :], (2 * SUBS, length))
        for group in range(LANES // (2 * SUBS)):
            shifted = both if group == 0 else roll_left(both, 2 * SUBS * group)
            shifted = shifted.astype(jnp.float32)
            for lag in range(2 * SUBS * group, window_len, LANES):
                skip = lag // LANES * LANES
                windows[comp * depth + lag:comp * depth + lag + 2 * SUBS, :] = (
                    shifted[:, skip:skip + length] * scale
                ).astype(jnp.bfloat16)

    total[...] += jnp.dot(units[...], windows[...], preferred_element_type=jnp.float32)

    @pl.when(step == pl.num_programs(0) - 1)
    def _():
        out[...] = total[...].T


def correlate(records, templates, moveouts, uptime):
    stations, components, length = records.shape
    _, _, window_len, bank = templates.shape
    depth = pl.cdiv(window_len, LANES) * LANES
    padded = length + depth
    counts = jnp.concatenate([moveouts.T, uptime.T], axis=0)
    return pl.pallas_call(
        functools.partial(correlate_kernel, uptime.shape[1]),
        out_shape=jax.ShapeDtypeStruct((length, bank), jnp.float32),
        grid_spec=pltpu.PrefetchScalarGridSpec(
            num_scalar_prefetch=1,
            grid=(stations,),
            in_specs=[
                pl.BlockSpec((components, stations, length), lambda s, *_: (0, 0, 0)),
                pl.BlockSpec((1, components, window_len, bank), lambda s, *_: (s, 0, 0, 0)),
            ],
            out_specs=pl.BlockSpec((length, bank), lambda s, *_: (0, 0)),
            scratch_shapes=[
                pltpu.VMEM((components, stations, length), jnp.float32),
                pltpu.VMEM((SUBS, padded), jnp.float32),
                pltpu.VMEM((components * depth, length), jnp.bfloat16),
                pltpu.VMEM((bank, components * depth), jnp.bfloat16),
                pltpu.VMEM((bank, length), jnp.float32),
            ],
        ),
        name="correlate",
    )(counts, records.transpose(1, 0, 2), templates)


def reduce_kernel(
    x_size, z_size, part, out, from_core, to_x, from_x, to_z, from_z,
    core_send, core_recv, x_send, x_recv, z_send, z_recv,
):
    tm, z = lax.axis_index("tm"), lax.axis_index("chan")
    x, core = lax.div(tm, 2), lax.rem(tm, 2)
    rows = part.shape[0] // (2 * x_size)
    piece = rows // z_size
    mesh_id = pl.DeviceIdType.MESH
    partner = 1 - core + 2 * x

    barrier = pltpu.get_barrier_semaphore()
    pl.semaphore_signal(barrier, inc=1, device_id={"tm": partner}, device_id_type=mesh_id)
    for d in range(1, x_size):
        peer = 2 * lax.rem(x + d, x_size) + core
        pl.semaphore_signal(barrier, inc=1, device_id={"tm": peer}, device_id_type=mesh_id)
    for e in range(1, z_size):
        peer = lax.rem(z + e, z_size)
        pl.semaphore_signal(barrier, inc=1, device_id={"chan": peer}, device_id_type=mesh_id)
    pl.semaphore_wait(barrier, x_size + z_size - 1)

    def start(src, dst, send, recv, device):
        copy = pltpu.make_async_remote_copy(
            src_ref=src, dst_ref=dst, send_sem=send, recv_sem=recv,
            device_id=device, device_id_type=mesh_id,
        )
        copy.start()
        return copy

    core_copies, x_copies, z_copies = [], [], []
    for d in range(1, x_size + 1):
        peer = lax.rem(x + d, x_size)
        first = pl.multiple_of((2 * peer + 1 - core) * rows, rows)
        core_copies.append(start(
            part.at[pl.ds(first, rows)], from_core.at[d - 1],
            core_send.at[d - 1], core_recv.at[d - 1], {"tm": partner},
        ))

    for d in range(1, x_size):
        peer = lax.rem(x + d, x_size)
        core_copies[d - 1].wait_recv()
        pending = []
        for e in range(1, z_size + 1):
            offset = pl.multiple_of(lax.rem(z + e, z_size) * piece, piece)
            first = pl.multiple_of((2 * peer + core) * rows + offset, piece)
            value = part[pl.ds(first, piece), :] + from_core[d - 1, pl.ds(offset, piece), :]
            to_x[d - 1, pl.ds(offset, piece), :] = value.astype(to_x.dtype)
            pending.append(start(
                to_x.at[d - 1, pl.ds(offset, piece)], from_x.at[d - 1, pl.ds(offset, piece)],
                x_send.at[d - 1, e - 1], x_recv.at[d - 1, e - 1], {"tm": 2 * peer + core},
            ))
        x_copies.append(pending)

    core_copies[x_size - 1].wait_recv()
    for e in range(1, z_size + 1):
        peer = lax.rem(z + e, z_size)
        offset = pl.multiple_of(peer * piece, piece)
        first = pl.multiple_of(tm * rows + offset, piece)
        value = part[pl.ds(first, piece), :] + from_core[x_size - 1, pl.ds(offset, piece), :]
        for d in range(1, x_size):
            x_copies[d - 1][e - 1].wait_recv()
            value = value + from_x[d - 1, pl.ds(offset, piece), :].astype(jnp.float32)
        if e < z_size:
            to_z[e - 1] = value.astype(to_z.dtype)
            z_copies.append(start(
                to_z.at[e - 1], from_z.at[e - 1], z_send.at[e - 1], z_recv.at[e - 1],
                {"chan": peer},
            ))
    for e in range(1, z_size):
        z_copies[e - 1].wait_recv()
        value = value + from_z[e - 1].astype(jnp.float32)
    out[...] = value

    for copy in core_copies + [c for pending in x_copies for c in pending] + z_copies:
        copy.wait_send()


def reduce_scatter(part):
    x_size, z_size = lax.axis_size("tm") // 2, lax.axis_size("chan")
    length, bank = part.shape
    rows = length // (2 * x_size)
    piece = rows // z_size
    others_x, others_z = max(x_size - 1, 1), max(z_size - 1, 1)
    dma = pltpu.SemaphoreType.DMA
    return pl.pallas_call(
        functools.partial(reduce_kernel, x_size, z_size),
        out_shape=jax.ShapeDtypeStruct((piece, bank), jnp.float32),
        in_specs=[pl.BlockSpec(memory_space=pltpu.VMEM)],
        out_specs=pl.BlockSpec(memory_space=pltpu.VMEM),
        scratch_shapes=[
            pltpu.VMEM((x_size, rows, bank), jnp.float32),
            pltpu.VMEM((others_x, rows, bank), jnp.bfloat16),
            pltpu.VMEM((others_x, rows, bank), jnp.bfloat16),
            pltpu.VMEM((others_z, piece, bank), jnp.bfloat16),
            pltpu.VMEM((others_z, piece, bank), jnp.bfloat16),
            dma((x_size,)), dma((x_size,)),
            dma((others_x, z_size)), dma((others_x, z_size)),
            dma((others_z,)), dma((others_z,)),
        ],
        compiler_params=pltpu.CompilerParams(collective_id=0, has_side_effects=True),
        name="reduce_scatter",
    )(part)


def body(records, templates, moveouts, uptime):
    return reduce_scatter(correlate(records, templates, moveouts, uptime)).T


def solution(mesh):
    placed = (
        P(("grp", "tm", "chan"), None, None),
        P(("tm", "chan"), None, None, None),
        P(("tm", "chan"), None),
        P(("grp", "tm", "chan"), None),
    )
    return jax.shard_map(
        body, mesh=mesh, in_specs=placed, out_specs=P(None, ("grp", "tm", "chan")), check_vma=False
    )
```

```python
import functools

import jax
import jax.numpy as jnp
from jax import lax
from jax.experimental import pallas as pl
from jax.experimental.pallas import tpu as pltpu
from jax.sharding import PartitionSpec as P

LANES = 128
SUBS = 8


def roll_left(value, amount):
    size = value.shape[-1]
    return pltpu.roll(value, (size - amount) % size, axis=1)


def windowed_sum(squares, window_len):
    total, covered, power, width = None, 0, squares, 1
    while width <= window_len:
        if window_len & width:
            piece = power if covered == 0 else roll_left(power, covered)
            total = piece if total is None else total + piece
            covered += width
        if 2 * width <= window_len:
            power = power + roll_left(power, width)
        width *= 2
    return total


def prepare(counts, records, signals, factors, window_len):
    components, stations, length = records.shape
    blocks = counts.shape[1] - components
    block_len = length // blocks
    time = lax.broadcasted_iota(jnp.int32, (stations, length), 1)
    limit = jnp.zeros((stations, length), jnp.int32)
    for block in range(blocks):
        live = block * block_len + counts[:, components + block:components + block + 1]
        limit = jnp.where(time >= block * block_len, live, limit)
    signals[...] = jnp.zeros_like(signals)
    for comp in range(components):
        row = jnp.where(time < limit, records[comp].astype(jnp.float32), 0.0)
        start = counts[:, comp:comp + 1]
        shift = 1
        while shift < length:
            row = jnp.where((start & shift) != 0, roll_left(row, shift), row)
            shift *= 2
        top = comp * stations
        signals[top:top + stations, :length] = jnp.where(time < length - start, row, 0.0)
        signal = signals[top:top + stations, :]
        energy = windowed_sum(signal * signal, window_len)
        factors[top:top + stations, :] = lax.rsqrt(jnp.maximum(energy[:, :length], 1.0))


def build(row, local, comp, templates, signals, factors, windows, units):
    window_len = templates.shape[2]
    depth, length = windows.shape
    padded = signals.shape[1]
    values = templates[local, comp].astype(jnp.float32)
    squares = jnp.sum(values * values, axis=0, keepdims=True)
    unit = (values * lax.rsqrt(squares + 1e-06)).astype(jnp.bfloat16)
    blank = jnp.zeros((depth - window_len, unit.shape[1]), unit.dtype)
    units[...] = jnp.concatenate([unit, blank], axis=0).T

    sub = lax.broadcasted_iota(jnp.int32, (SUBS, padded), 0)
    base = jnp.broadcast_to(signals[pl.ds(row, 1), :], (SUBS, padded))
    for bit in (1, 2, 4):
        base = jnp.where((sub & bit) != 0, roll_left(base, bit), base)
    both = jnp.concatenate([base, roll_left(base, SUBS)], axis=0).astype(jnp.bfloat16)
    scale = jnp.broadcast_to(factors[pl.ds(row, 1), :], (2 * SUBS, length))
    for group in range(LANES // (2 * SUBS)):
        shifted = both if group == 0 else roll_left(both, 2 * SUBS * group)
        shifted = shifted.astype(jnp.float32)
        for lag in range(2 * SUBS * group, window_len, LANES):
            skip = lag // LANES * LANES
            windows[lag:lag + 2 * SUBS, :] = (
                shifted[:, skip:skip + length] * scale
            ).astype(jnp.bfloat16)


def correlate_kernel(group, counts, records, templates, out, signals, factors, total, *scratch):
    step = pl.program_id(0)
    components, stations, _ = records.shape
    slots = group * components
    windows, units = scratch[:slots], scratch[slots:]

    def product(slot):
        return jnp.dot(units[slot][...], windows[slot][...], preferred_element_type=jnp.float32)

    @pl.when(step == 0)
    def _():
        prepare(counts, records, signals, factors, templates.shape[2])
        total[...] = jnp.zeros_like(total)
        for ref in scratch:
            ref[...] = jnp.zeros_like(ref)

    for slot in range(slots):
        local, comp = slot // components, slot % components
        row = comp * stations + step * group + local
        build(row, local, comp, templates, signals, factors, windows[slot], units[slot])
    total[...] += sum(product(slot) for slot in range(slots))

    @pl.when(step == pl.num_programs(0) - 1)
    def _():
        out[...] = total[...].T


def correlate(records, templates, moveouts, uptime):
    stations, components, length = records.shape
    _, _, window_len, bank = templates.shape
    depth = pl.cdiv(window_len, LANES) * LANES
    padded = length + depth
    counts = jnp.concatenate([moveouts, uptime], axis=1)
    group = 1
    slots = group * components
    return pl.pallas_call(
        functools.partial(correlate_kernel, group),
        out_shape=jax.ShapeDtypeStruct((length, bank), jnp.float32),
        grid=(stations // group,),
        in_specs=[
            pl.BlockSpec(counts.shape, lambda s: (0, 0)),
            pl.BlockSpec((components, stations, length), lambda s: (0, 0, 0)),
            pl.BlockSpec((group, components, window_len, bank), lambda s: (s, 0, 0, 0)),
        ],
        out_specs=pl.BlockSpec((length, bank), lambda s: (0, 0)),
        scratch_shapes=[
            pltpu.VMEM((components * stations, padded), jnp.float32),
            pltpu.VMEM((components * stations, length), jnp.float32),
            pltpu.VMEM((bank, length), jnp.float32),
        ]
        + [pltpu.VMEM((depth, length), jnp.bfloat16)] * slots
        + [pltpu.VMEM((bank, depth), jnp.bfloat16)] * slots,
        compiler_params=pltpu.CompilerParams(),
        name="correlate",
    )(counts, records.transpose(1, 0, 2), templates)


def reduce_kernel(
    x_size, z_size, part, out, from_core, to_x, from_x, to_z, from_z,
    core_send, core_recv, x_send, x_recv, z_send, z_recv,
):
    tm, z = lax.axis_index("tm"), lax.axis_index("chan")
    x, core = lax.div(tm, 2), lax.rem(tm, 2)
    rows = part.shape[0] // (2 * x_size)
    piece = rows // z_size
    mesh_id = pl.DeviceIdType.MESH
    partner = 1 - core + 2 * x

    barrier = pltpu.get_barrier_semaphore()
    pl.semaphore_signal(barrier, inc=1, device_id={"tm": partner}, device_id_type=mesh_id)
    for d in range(1, x_size):
        peer = 2 * lax.rem(x + d, x_size) + core
        pl.semaphore_signal(barrier, inc=1, device_id={"tm": peer}, device_id_type=mesh_id)
    for e in range(1, z_size):
        peer = lax.rem(z + e, z_size)
        pl.semaphore_signal(barrier, inc=1, device_id={"chan": peer}, device_id_type=mesh_id)
    pl.semaphore_wait(barrier, x_size + z_size - 1)

    def start(src, dst, send, recv, device):
        copy = pltpu.make_async_remote_copy(
            src_ref=src, dst_ref=dst, send_sem=send, recv_sem=recv,
            device_id=device, device_id_type=mesh_id,
        )
        copy.start()
        return copy

    core_copies, x_copies, z_copies = [], [], []
    for d in range(1, x_size + 1):
        peer = lax.rem(x + d, x_size)
        pending = []
        for e in range(1, z_size + 1):
            offset = pl.multiple_of(lax.rem(z + e, z_size) * piece, piece)
            first = pl.multiple_of((2 * peer + 1 - core) * rows + offset, piece)
            pending.append(start(
                part.at[pl.ds(first, piece)], from_core.at[d - 1, pl.ds(offset, piece)],
                core_send.at[d - 1, e - 1], core_recv.at[d - 1, e - 1], {"tm": partner},
            ))
        core_copies.append(pending)

    for d in range(1, x_size):
        peer = lax.rem(x + d, x_size)
        pending = []
        for e in range(1, z_size + 1):
            core_copies[d - 1][e - 1].wait_recv()
            offset = pl.multiple_of(lax.rem(z + e, z_size) * piece, piece)
            first = pl.multiple_of((2 * peer + core) * rows + offset, piece)
            value = part[pl.ds(first, piece), :] + from_core[d - 1, pl.ds(offset, piece), :]
            to_x[d - 1, pl.ds(offset, piece), :] = value.astype(to_x.dtype)
            pending.append(start(
                to_x.at[d - 1, pl.ds(offset, piece)], from_x.at[d - 1, pl.ds(offset, piece)],
                x_send.at[d - 1, e - 1], x_recv.at[d - 1, e - 1], {"tm": 2 * peer + core},
            ))
        x_copies.append(pending)

    for e in range(1, z_size + 1):
        core_copies[x_size - 1][e - 1].wait_recv()
        peer = lax.rem(z + e, z_size)
        offset = pl.multiple_of(peer * piece, piece)
        first = pl.multiple_of(tm * rows + offset, piece)
        value = part[pl.ds(first, piece), :] + from_core[x_size - 1, pl.ds(offset, piece), :]
        for d in range(1, x_size):
            x_copies[d - 1][e - 1].wait_recv()
            value = value + from_x[d - 1, pl.ds(offset, piece), :].astype(jnp.float32)
        if e < z_size:
            to_z[e - 1] = value.astype(to_z.dtype)
            z_copies.append(start(
                to_z.at[e - 1], from_z.at[e - 1], z_send.at[e - 1], z_recv.at[e - 1],
                {"chan": peer},
            ))
    for e in range(1, z_size):
        z_copies[e - 1].wait_recv()
        value = value + from_z[e - 1].astype(jnp.float32)
    out[...] = value

    for copy in sum(core_copies + x_copies, []) + z_copies:
        copy.wait_send()


def reduce_scatter(part):
    x_size, z_size = lax.axis_size("tm") // 2, lax.axis_size("chan")
    length, bank = part.shape
    rows = length // (2 * x_size)
    piece = rows // z_size
    others_x, others_z = max(x_size - 1, 1), max(z_size - 1, 1)
    dma = pltpu.SemaphoreType.DMA
    return pl.pallas_call(
        functools.partial(reduce_kernel, x_size, z_size),
        out_shape=jax.ShapeDtypeStruct((piece, bank), jnp.float32),
        in_specs=[pl.BlockSpec(memory_space=pltpu.VMEM)],
        out_specs=pl.BlockSpec(memory_space=pltpu.VMEM),
        scratch_shapes=[
            pltpu.VMEM((x_size, rows, bank), jnp.float32),
            pltpu.VMEM((others_x, rows, bank), jnp.bfloat16),
            pltpu.VMEM((others_x, rows, bank), jnp.bfloat16),
            pltpu.VMEM((others_z, piece, bank), jnp.bfloat16),
            pltpu.VMEM((others_z, piece, bank), jnp.bfloat16),
            dma((x_size, z_size)), dma((x_size, z_size)),
            dma((others_x, z_size)), dma((others_x, z_size)),
            dma((others_z,)), dma((others_z,)),
        ],
        compiler_params=pltpu.CompilerParams(collective_id=0, has_side_effects=True),
        name="reduce_scatter",
    )(part)


def body(records, templates, moveouts, uptime):
    return reduce_scatter(correlate(records, templates, moveouts, uptime)).T


def solution(mesh):
    placed = (
        P(("grp", "tm", "chan"), None, None),
        P(("tm", "chan"), None, None, None),
        P(("tm", "chan"), None),
        P(("grp", "tm", "chan"), None),
    )
    return jax.shard_map(
        body, mesh=mesh, in_specs=placed, out_specs=P(None, ("grp", "tm", "chan")), check_vma=False
    )
```

```python
import functools

import jax
import jax.numpy as jnp
from jax import lax
from jax.experimental import pallas as pl
from jax.experimental.pallas import tpu as pltpu
from jax.sharding import PartitionSpec as P

LANES = 128
SUBS = 8


def roll_left(value, amount):
    size = value.shape[-1]
    return pltpu.roll(value, (size - amount) % size, axis=1)


def windowed_sum(squares, window_len):
    powers, power, width = [], squares, 1
    while width <= window_len:
        if window_len & width:
            powers.append((width, power))
        if 2 * width <= window_len:
            power = power + roll_left(power, width)
        width *= 2
    covered, total = powers[-1]
    for width, power in powers[-2::-1]:
        total = total + roll_left(power, covered)
        covered += width
    return total


def prepare(counts_ref, records, signals, factors, window_len):
    components, stations, length = records.shape
    counts = counts_ref[...].T
    blocks = counts.shape[1] - components
    block_len = length // blocks
    time = lax.broadcasted_iota(jnp.int32, (stations, length), 1)
    limit = jnp.zeros((stations, length), jnp.int32)
    for block in range(blocks):
        live = block * block_len + counts[:, components + block:components + block + 1]
        limit = jnp.where(time >= block * block_len, live, limit)
    signals[...] = jnp.zeros_like(signals)
    for comp in range(components):
        row = jnp.where(time < limit, records[comp].astype(jnp.float32), 0.0)
        start = counts[:, comp:comp + 1]
        shift = 1
        while shift < length:
            row = jnp.where((start & shift) != 0, roll_left(row, shift), row)
            shift *= 2
        top = comp * stations
        signals[top:top + stations, :length] = jnp.where(time < length - start, row, 0.0)
        signal = signals[top:top + stations, :]
        energy = windowed_sum(signal * signal, window_len)
        factors[top:top + stations, :] = lax.rsqrt(jnp.maximum(energy[:, :length], 1.0))


def spread(row, signals):
    padded = signals.shape[1]
    sub = lax.broadcasted_iota(jnp.int32, (SUBS, padded), 0)
    base = jnp.broadcast_to(signals[pl.ds(row, 1), :], (SUBS, padded))
    for bit in (1, 2, 4):
        base = jnp.where((sub & bit) != 0, roll_left(base, bit), base)
    return jnp.concatenate([base, roll_left(base, SUBS)], axis=0).astype(jnp.bfloat16)


def build(row, local, comp, templates, both, factors, windows, units):
    window_len = templates.shape[2]
    depth, length = windows.shape
    values = templates[local, comp].astype(jnp.float32)
    squares = jnp.sum(values * values, axis=0, keepdims=True)
    unit = (values * lax.rsqrt(squares + 1e-06)).astype(jnp.bfloat16)
    blank = jnp.zeros((depth - window_len, unit.shape[1]), unit.dtype)
    units[...] = jnp.concatenate([unit, blank], axis=0).T

    scale = jnp.broadcast_to(factors[pl.ds(row, 1), :], (2 * SUBS, length))
    for group in range(LANES // (2 * SUBS)):
        shifted = both if group == 0 else roll_left(both, 2 * SUBS * group)
        shifted = shifted.astype(jnp.float32)
        for lag in range(2 * SUBS * group, window_len, LANES):
            skip = lag // LANES * LANES
            windows[lag:lag + 2 * SUBS, :] = (
                shifted[:, skip:skip + length] * scale
            ).astype(jnp.bfloat16)


def correlate_kernel(group, counts, records, templates, out, signals, factors, total, *scratch):
    step = pl.program_id(0)
    components, stations, _ = records.shape
    slots = group * components
    windows, units, bases = scratch[:slots], scratch[slots:2 * slots], scratch[2 * slots:]

    def product(slot):
        return jnp.dot(units[slot][...], windows[slot][...], preferred_element_type=jnp.float32)

    @pl.when(step == 0)
    def _():
        prepare(counts, records, signals, factors, templates.shape[2])
        total[...] = jnp.zeros_like(total)
        for ref in windows + units:
            ref[...] = jnp.zeros_like(ref)
        for comp in range(components):
            bases[comp][...] = spread(comp * stations, signals)

    following = jnp.minimum(step + 1, stations - 1)
    for comp in range(components):
        row = comp * stations + step
        build(row, 0, comp, templates, bases[comp][...], factors, windows[comp], units[comp])
        bases[comp][...] = spread(comp * stations + following, signals)
    total[...] += sum(product(slot) for slot in range(slots))

    @pl.when(step == pl.num_programs(0) - 1)
    def _():
        out[...] = total[...].T


def correlate(records, templates, moveouts, uptime):
    stations, components, length = records.shape
    _, _, window_len, bank = templates.shape
    depth = pl.cdiv(window_len, LANES) * LANES
    padded = length + depth
    counts = jnp.concatenate([moveouts.T, uptime.T], axis=0)
    group = 1
    slots = group * components
    return pl.pallas_call(
        functools.partial(correlate_kernel, group),
        out_shape=jax.ShapeDtypeStruct((length, bank), jnp.float32),
        grid=(stations // group,),
        in_specs=[
            pl.BlockSpec(counts.shape, lambda s: (0, 0)),
            pl.BlockSpec((components, stations, length), lambda s: (0, 0, 0)),
            pl.BlockSpec((group, components, window_len, bank), lambda s: (s, 0, 0, 0)),
        ],
        out_specs=pl.BlockSpec((length, bank), lambda s: (0, 0)),
        scratch_shapes=[
            pltpu.VMEM((components * stations, padded), jnp.float32),
            pltpu.VMEM((components * stations, length), jnp.float32),
            pltpu.VMEM((bank, length), jnp.float32),
        ]
        + [pltpu.VMEM((depth, length), jnp.bfloat16)] * slots
        + [pltpu.VMEM((bank, depth), jnp.bfloat16)] * slots
        + [pltpu.VMEM((2 * SUBS, padded), jnp.bfloat16)] * slots,
        compiler_params=pltpu.CompilerParams(),
        name="correlate",
    )(counts, records.transpose(1, 0, 2), templates)


def reduce_kernel(
    x_size, z_size, part, out, from_core, to_x, from_x, to_z, from_z,
    core_send, core_recv, x_send, x_recv, z_send, z_recv,
):
    tm, z = lax.axis_index("tm"), lax.axis_index("chan")
    x, core = lax.div(tm, 2), lax.rem(tm, 2)
    rows = part.shape[0] // (2 * x_size)
    piece = rows // z_size
    mesh_id = pl.DeviceIdType.MESH
    partner = 1 - core + 2 * x

    barrier = pltpu.get_barrier_semaphore()
    pl.semaphore_signal(barrier, inc=1, device_id={"tm": partner}, device_id_type=mesh_id)
    for d in range(1, x_size):
        peer = 2 * lax.rem(x + d, x_size) + core
        pl.semaphore_signal(barrier, inc=1, device_id={"tm": peer}, device_id_type=mesh_id)
    for e in range(1, z_size):
        peer = lax.rem(z + e, z_size)
        pl.semaphore_signal(barrier, inc=1, device_id={"chan": peer}, device_id_type=mesh_id)
    pl.semaphore_wait(barrier, x_size + z_size - 1)

    def start(src, dst, send, recv, device):
        copy = pltpu.make_async_remote_copy(
            src_ref=src, dst_ref=dst, send_sem=send, recv_sem=recv,
            device_id=device, device_id_type=mesh_id,
        )
        copy.start()
        return copy

    core_copies, x_copies, z_copies = [], [], []
    for d in range(1, x_size + 1):
        peer = lax.rem(x + d, x_size)
        pending = []
        for e in range(1, z_size + 1):
            offset = pl.multiple_of(lax.rem(z + e, z_size) * piece, piece)
            first = pl.multiple_of((2 * peer + 1 - core) * rows + offset, piece)
            pending.append(start(
                part.at[pl.ds(first, piece)], from_core.at[d - 1, pl.ds(offset, piece)],
                core_send.at[d - 1, e - 1], core_recv.at[d - 1, e - 1], {"tm": partner},
            ))
        core_copies.append(pending)

    for d in range(1, x_size):
        peer = lax.rem(x + d, x_size)
        pending = []
        for e in range(1, z_size + 1):
            core_copies[d - 1][e - 1].wait_recv()
            offset = pl.multiple_of(lax.rem(z + e, z_size) * piece, piece)
            first = pl.multiple_of((2 * peer + core) * rows + offset, piece)
            value = part[pl.ds(first, piece), :] + from_core[d - 1, pl.ds(offset, piece), :]
            to_x[d - 1, pl.ds(offset, piece), :] = value.astype(to_x.dtype)
            pending.append(start(
                to_x.at[d - 1, pl.ds(offset, piece)], from_x.at[d - 1, pl.ds(offset, piece)],
                x_send.at[d - 1, e - 1], x_recv.at[d - 1, e - 1], {"tm": 2 * peer + core},
            ))
        x_copies.append(pending)

    for e in range(1, z_size + 1):
        core_copies[x_size - 1][e - 1].wait_recv()
        peer = lax.rem(z + e, z_size)
        offset = pl.multiple_of(peer * piece, piece)
        first = pl.multiple_of(tm * rows + offset, piece)
        value = part[pl.ds(first, piece), :] + from_core[x_size - 1, pl.ds(offset, piece), :]
        for d in range(1, x_size):
            x_copies[d - 1][e - 1].wait_recv()
            value = value + from_x[d - 1, pl.ds(offset, piece), :].astype(jnp.float32)
        if e < z_size:
            to_z[e - 1] = value.astype(to_z.dtype)
            z_copies.append(start(
                to_z.at[e - 1], from_z.at[e - 1], z_send.at[e - 1], z_recv.at[e - 1],
                {"chan": peer},
            ))
    for e in range(1, z_size):
        z_copies[e - 1].wait_recv()
        value = value + from_z[e - 1].astype(jnp.float32)
    out[...] = value

    for copy in sum(core_copies + x_copies, []) + z_copies:
        copy.wait_send()


def reduce_scatter(part):
    x_size, z_size = lax.axis_size("tm") // 2, lax.axis_size("chan")
    length, bank = part.shape
    rows = length // (2 * x_size)
    piece = rows // z_size
    others_x, others_z = max(x_size - 1, 1), max(z_size - 1, 1)
    dma = pltpu.SemaphoreType.DMA
    return pl.pallas_call(
        functools.partial(reduce_kernel, x_size, z_size),
        out_shape=jax.ShapeDtypeStruct((piece, bank), jnp.float32),
        in_specs=[pl.BlockSpec(memory_space=pltpu.VMEM)],
        out_specs=pl.BlockSpec(memory_space=pltpu.VMEM),
        scratch_shapes=[
            pltpu.VMEM((x_size, rows, bank), jnp.float32),
            pltpu.VMEM((others_x, rows, bank), jnp.bfloat16),
            pltpu.VMEM((others_x, rows, bank), jnp.bfloat16),
            pltpu.VMEM((others_z, piece, bank), jnp.bfloat16),
            pltpu.VMEM((others_z, piece, bank), jnp.bfloat16),
            dma((x_size, z_size)), dma((x_size, z_size)),
            dma((others_x, z_size)), dma((others_x, z_size)),
            dma((others_z,)), dma((others_z,)),
        ],
        compiler_params=pltpu.CompilerParams(collective_id=0, has_side_effects=True),
        name="reduce_scatter",
    )(part)


def body(records, templates, moveouts, uptime):
    return reduce_scatter(correlate(records, templates, moveouts, uptime)).T


def solution(mesh):
    placed = (
        P(("grp", "tm", "chan"), None, None),
        P(("tm", "chan"), None, None, None),
        P(("tm", "chan"), None),
        P(("grp", "tm", "chan"), None),
    )
    return jax.shard_map(
        body, mesh=mesh, in_specs=placed, out_specs=P(None, ("grp", "tm", "chan")), check_vma=False
    )
```

```python
import functools

import jax
import jax.numpy as jnp
from jax import lax
from jax.experimental import pallas as pl
from jax.experimental.pallas import tpu as pltpu
from jax.sharding import PartitionSpec as P

LANES = 128
SUBS = 8


def roll_left(value, amount):
    size = value.shape[-1]
    return pltpu.roll(value, (size - amount) % size, axis=1)


def windowed_sum(squares, window_len):
    powers, power, width = [], squares, 1
    while width <= window_len:
        if window_len & width:
            powers.append((width, power))
        if 2 * width <= window_len:
            power = power + roll_left(power, width)
        width *= 2
    covered, total = powers[-1]
    for width, power in powers[-2::-1]:
        total = total + roll_left(power, covered)
        covered += width
    return total


def prepare(counts_ref, records, signals, factors, window_len):
    components, stations, length = records.shape
    counts = counts_ref[...].T
    blocks = counts.shape[1] - components
    block_len = length // blocks
    time = lax.broadcasted_iota(jnp.int32, (stations, length), 1)
    limit = jnp.zeros((stations, length), jnp.int32)
    for block in range(blocks):
        live = block * block_len + counts[:, components + block:components + block + 1]
        limit = jnp.where(time >= block * block_len, live, limit)
    signals[...] = jnp.zeros_like(signals)
    for comp in range(components):
        row = jnp.where(time < limit, records[comp].astype(jnp.float32), 0.0)
        start = counts[:, comp:comp + 1]
        shift = 1
        while shift < length:
            row = jnp.where((start & shift) != 0, roll_left(row, shift), row)
            shift *= 2
        top = comp * stations
        signals[top:top + stations, :length] = jnp.where(time < length - start, row, 0.0)
        signal = signals[top:top + stations, :]
        energy = windowed_sum(signal * signal, window_len)
        factors[top:top + stations, :] = lax.rsqrt(jnp.maximum(energy[:, :length], 1.0))


def spread(row, signals):
    padded = signals.shape[1]
    sub = lax.broadcasted_iota(jnp.int32, (SUBS, padded), 0)
    base = jnp.broadcast_to(signals[pl.ds(row, 1), :], (SUBS, padded))
    for bit in (1, 2, 4):
        base = jnp.where((sub & bit) != 0, roll_left(base, bit), base)
    return jnp.concatenate([base, roll_left(base, SUBS)], axis=0).astype(jnp.bfloat16)


def build(row, local, comp, templates, both, factors, windows, units):
    window_len = templates.shape[2]
    depth, length = windows.shape
    values = templates[local, comp].astype(jnp.float32)
    squares = jnp.sum(values * values, axis=0, keepdims=True)
    unit = (values * lax.rsqrt(squares + 1e-06)).astype(jnp.bfloat16)
    blank = jnp.zeros((depth - window_len, unit.shape[1]), unit.dtype)
    units[...] = jnp.concatenate([unit, blank], axis=0).T

    scale = jnp.broadcast_to(factors[pl.ds(row, 1), :], (2 * SUBS, length))
    for group in range(LANES // (2 * SUBS)):
        shifted = both if group == 0 else roll_left(both, 2 * SUBS * group)
        shifted = shifted.astype(jnp.float32)
        for lag in range(2 * SUBS * group, window_len, LANES):
            skip = lag // LANES * LANES
            windows[lag:lag + 2 * SUBS, :] = (
                shifted[:, skip:skip + length] * scale
            ).astype(jnp.bfloat16)


def correlate_kernel(group, counts, records, templates, out, signals, factors, total, *scratch):
    step = pl.program_id(0)
    components, stations, _ = records.shape
    slots = group * components
    windows, units, bases = scratch[:slots], scratch[slots:2 * slots], scratch[2 * slots:]

    def product(slot):
        return jnp.dot(units[slot][...], windows[slot][...], preferred_element_type=jnp.float32)

    @pl.when(step == 0)
    def _():
        prepare(counts, records, signals, factors, templates.shape[2])
        total[...] = jnp.zeros_like(total)
        for ref in windows + units:
            ref[...] = jnp.zeros_like(ref)
        for comp in range(components):
            bases[comp][...] = spread(comp * stations, signals)

    following = jnp.minimum(step + 1, stations - 1)
    for comp in range(components):
        row = comp * stations + step
        build(row, 0, comp, templates, bases[comp][...], factors, windows[comp], units[comp])
        bases[comp][...] = spread(comp * stations + following, signals)
    total[...] += sum(product(slot) for slot in range(slots))

    @pl.when(step == pl.num_programs(0) - 1)
    def _():
        out[...] = total[...].T.astype(out.dtype)


def correlate(records, templates, moveouts, uptime):
    stations, components, length = records.shape
    _, _, window_len, bank = templates.shape
    depth = pl.cdiv(window_len, LANES) * LANES
    padded = length + depth
    counts = jnp.concatenate([moveouts.T, uptime.T], axis=0)
    group = 1
    slots = group * components
    return pl.pallas_call(
        functools.partial(correlate_kernel, group),
        out_shape=jax.ShapeDtypeStruct((length, bank), jnp.bfloat16),
        grid=(stations // group,),
        in_specs=[
            pl.BlockSpec(counts.shape, lambda s: (0, 0)),
            pl.BlockSpec((components, stations, length), lambda s: (0, 0, 0)),
            pl.BlockSpec((group, components, window_len, bank), lambda s: (s, 0, 0, 0)),
        ],
        out_specs=pl.BlockSpec((length, bank), lambda s: (0, 0)),
        scratch_shapes=[
            pltpu.VMEM((components * stations, padded), jnp.float32),
            pltpu.VMEM((components * stations, length), jnp.float32),
            pltpu.VMEM((bank, length), jnp.float32),
        ]
        + [pltpu.VMEM((depth, length), jnp.bfloat16)] * slots
        + [pltpu.VMEM((bank, depth), jnp.bfloat16)] * slots
        + [pltpu.VMEM((2 * SUBS, padded), jnp.bfloat16)] * slots,
        compiler_params=pltpu.CompilerParams(),
        name="correlate",
    )(counts, records.transpose(1, 0, 2), templates)


def reduce_kernel(
    x_size, z_size, part, out, from_core, to_x, from_x, to_z, from_z,
    core_send, core_recv, x_send, x_recv, z_send, z_recv,
):
    tm, z = lax.axis_index("tm"), lax.axis_index("chan")
    x, core = lax.div(tm, 2), lax.rem(tm, 2)
    rows = part.shape[0] // (2 * x_size)
    piece = rows // z_size
    mesh_id = pl.DeviceIdType.MESH
    partner = 1 - core + 2 * x

    barrier = pltpu.get_barrier_semaphore()
    pl.semaphore_signal(barrier, inc=1, device_id={"tm": partner}, device_id_type=mesh_id)
    for d in range(1, x_size):
        peer = 2 * lax.rem(x + d, x_size) + core
        pl.semaphore_signal(barrier, inc=1, device_id={"tm": peer}, device_id_type=mesh_id)
    for e in range(1, z_size):
        peer = lax.rem(z + e, z_size)
        pl.semaphore_signal(barrier, inc=1, device_id={"chan": peer}, device_id_type=mesh_id)
    pl.semaphore_wait(barrier, x_size + z_size - 1)

    def start(src, dst, send, recv, device):
        copy = pltpu.make_async_remote_copy(
            src_ref=src, dst_ref=dst, send_sem=send, recv_sem=recv,
            device_id=device, device_id_type=mesh_id,
        )
        copy.start()
        return copy

    core_copies, x_copies, z_copies = [], [], []
    for d in range(1, x_size + 1):
        peer = lax.rem(x + d, x_size)
        pending = []
        for e in range(1, z_size + 1):
            offset = pl.multiple_of(lax.rem(z + e, z_size) * piece, piece)
            first = pl.multiple_of((2 * peer + 1 - core) * rows + offset, piece)
            pending.append(start(
                part.at[pl.ds(first, piece)], from_core.at[d - 1, pl.ds(offset, piece)],
                core_send.at[d - 1, e - 1], core_recv.at[d - 1, e - 1], {"tm": partner},
            ))
        core_copies.append(pending)

    for d in range(1, x_size):
        peer = lax.rem(x + d, x_size)
        pending = []
        for e in range(1, z_size + 1):
            core_copies[d - 1][e - 1].wait_recv()
            offset = pl.multiple_of(lax.rem(z + e, z_size) * piece, piece)
            first = pl.multiple_of((2 * peer + core) * rows + offset, piece)
            value = part[pl.ds(first, piece), :].astype(jnp.float32)
            value = value + from_core[d - 1, pl.ds(offset, piece), :].astype(jnp.float32)
            to_x[d - 1, pl.ds(offset, piece), :] = value.astype(to_x.dtype)
            pending.append(start(
                to_x.at[d - 1, pl.ds(offset, piece)], from_x.at[d - 1, pl.ds(offset, piece)],
                x_send.at[d - 1, e - 1], x_recv.at[d - 1, e - 1], {"tm": 2 * peer + core},
            ))
        x_copies.append(pending)

    for e in range(1, z_size + 1):
        core_copies[x_size - 1][e - 1].wait_recv()
        peer = lax.rem(z + e, z_size)
        offset = pl.multiple_of(peer * piece, piece)
        first = pl.multiple_of(tm * rows + offset, piece)
        value = part[pl.ds(first, piece), :].astype(jnp.float32)
        value = value + from_core[x_size - 1, pl.ds(offset, piece), :].astype(jnp.float32)
        for d in range(1, x_size):
            x_copies[d - 1][e - 1].wait_recv()
            value = value + from_x[d - 1, pl.ds(offset, piece), :].astype(jnp.float32)
        if e < z_size:
            to_z[e - 1] = value.astype(to_z.dtype)
            z_copies.append(start(
                to_z.at[e - 1], from_z.at[e - 1], z_send.at[e - 1], z_recv.at[e - 1],
                {"chan": peer},
            ))
    for e in range(1, z_size):
        z_copies[e - 1].wait_recv()
        value = value + from_z[e - 1].astype(jnp.float32)
    out[...] = value

    for copy in sum(core_copies + x_copies, []) + z_copies:
        copy.wait_send()


def reduce_scatter(part):
    x_size, z_size = lax.axis_size("tm") // 2, lax.axis_size("chan")
    length, bank = part.shape
    rows = length // (2 * x_size)
    piece = rows // z_size
    others_x, others_z = max(x_size - 1, 1), max(z_size - 1, 1)
    dma = pltpu.SemaphoreType.DMA
    return pl.pallas_call(
        functools.partial(reduce_kernel, x_size, z_size),
        out_shape=jax.ShapeDtypeStruct((piece, bank), jnp.float32),
        in_specs=[pl.BlockSpec(memory_space=pltpu.VMEM)],
        out_specs=pl.BlockSpec(memory_space=pltpu.VMEM),
        scratch_shapes=[
            pltpu.VMEM((x_size, rows, bank), part.dtype),
            pltpu.VMEM((others_x, rows, bank), jnp.bfloat16),
            pltpu.VMEM((others_x, rows, bank), jnp.bfloat16),
            pltpu.VMEM((others_z, piece, bank), jnp.bfloat16),
            pltpu.VMEM((others_z, piece, bank), jnp.bfloat16),
            dma((x_size, z_size)), dma((x_size, z_size)),
            dma((others_x, z_size)), dma((others_x, z_size)),
            dma((others_z,)), dma((others_z,)),
        ],
        compiler_params=pltpu.CompilerParams(collective_id=0, has_side_effects=True),
        name="reduce_scatter",
    )(part)


def body(records, templates, moveouts, uptime):
    return reduce_scatter(correlate(records, templates, moveouts, uptime)).T


def solution(mesh):
    placed = (
        P(("grp", "tm", "chan"), None, None),
        P(("tm", "chan"), None, None, None),
        P(("tm", "chan"), None),
        P(("grp", "tm", "chan"), None),
    )
    return jax.shard_map(
        body, mesh=mesh, in_specs=placed, out_specs=P(None, ("grp", "tm", "chan")), check_vma=False
    )
```
